32 devices in a mesh: bx: 8 (over z, y), by: 4 (over x, core).
Axes of the slice: x: 2, y: 2, z: 4, core: 2. Of those that a mesh axis runs over, the one named last changes fastest.
Arguments:
- polarization: float32 [3, 8, 256, 512], P(None, None, 'bx', 'by'), may hold values from -1.6 to 1.6
- alpha_field: float32 [8, 256, 512], P(None, 'bx', 'by'), may hold values from -1 to 1
- landau: float32 [3, 8], replicated, may hold values from 0.05 to 0.25
- stiffness: float32 [8], replicated, may hold values from 0.5 to 1.5
- permittivity: float32 [8], replicated, may hold values from 0.5 to 2
- interfaces: float32 [9], replicated, may hold values from 0.0002 to 0.0008
Outputs:
- polar_next: float32 [3, 8, 256, 512], P(None, None, 'bx', 'by')
- depol_field: float32 [3, 8, 256, 512], P(None, None, 'bx', 'by')
The draws below stay inside these ranges and needn't reach their ends.
All inputs are finite; a program needn't handle non-finite values.
Results may differ from the reference program's by a relative error of at most 0.0003.
Values sent between devices are 32-bit elements; how exact they have to be, the bound alone decides.
A program may use at most 64 MiB of HBM per device.

```python
import math
import jax
import jax.numpy as jnp
from jax import lax

LAYERS = 8
STEPS = 2
NX = 256
NY = 512


def draw_polarization(key, part):
    return 0.5 * jax.random.truncated_normal(key, -3.2, 3.2, (3, LAYERS, NX, NY), jnp.float32)


def shard_levels(stream_key, shape, pieces, least, top_value):
    factor_of, own = 1.0, jax.random.fold_in(stream_key, 6)
    for axis_at, blocks in pieces:
        draws = jnp.exp(jax.random.uniform(jax.random.fold_in(own, axis_at), (blocks,), jnp.float32, least / len(pieces), top_value / len(pieces)))
        factor_of = factor_of * jnp.repeat(draws, shape[axis_at] // blocks).reshape([-1 if axis == axis_at else 1 for axis in range(len(shape))])
    return factor_of


def setup_inputs(seed: int = 0) -> dict:
    key_of = jax.random.split(jax.random.key(seed), 7)
    return {
        "polarization": draw_polarization(jax.random.fold_in(key_of[6], 71), 0),
        "alpha_field": jnp.clip(jax.random.uniform(key_of[1], (LAYERS, NX, NY), jnp.float32, -1.0, 1.0) * shard_levels(key_of[1], (LAYERS, NX, NY), ((1, 8), (2, 4)), -0.4, 0.0), -1.0, 1.0),
        "landau": jnp.clip(jax.random.uniform(key_of[2], (3, LAYERS), jnp.float32, 0.05, 0.25), 0.05, 0.25),
        "stiffness": jnp.clip(jax.random.uniform(key_of[3], (LAYERS,), jnp.float32, 0.5, 1.5), 0.5, 1.5),
        "permittivity": jnp.clip(jnp.exp(jax.random.uniform(key_of[4], (LAYERS,), jnp.float32, math.log(0.5), math.log(2.0))), 0.5, 2.0),
        "interfaces": jnp.clip(jnp.exp(jax.random.uniform(key_of[5], (LAYERS + 1,), jnp.float32, math.log(0.0002), math.log(0.0008))), 0.0002, 0.0008),
    }


step_size = 0.05


def shift_up(source, axis_no):
    upper_part = lax.slice_in_dim(source, 1, source.shape[axis_no], axis=axis_no)
    return jnp.concatenate([upper_part, jnp.zeros_like(lax.slice_in_dim(source, 0, 1, axis=axis_no))], axis=axis_no)


def shift_down(source, axis_no):
    lower_part = lax.slice_in_dim(source, 0, source.shape[axis_no] - 1, axis=axis_no)
    return jnp.concatenate([jnp.zeros_like(lax.slice_in_dim(source, 0, 1, axis=axis_no)), lower_part], axis=axis_no)


def central(source, axis_no):
    return 0.5 * (jnp.roll(source, -1, axis_no) - jnp.roll(source, 1, axis_no))


def depolarize(polar_now, permittivity, interfaces):
    charge = -(central(polar_now[0], 1) + central(polar_now[1], 2)
               + 0.5 * (shift_up(polar_now[2], 0) - shift_down(polar_now[2], 0)))
    spectrum = jnp.fft.fft2(charge)
    layers = charge.shape[0]
    grid_x = charge.shape[1]
    grid_y = charge.shape[2]
    wave_x = jnp.sin(jnp.pi * jnp.arange(grid_x).astype(jnp.float32) / grid_x)
    wave_y = jnp.sin(jnp.pi * jnp.arange(grid_y).astype(jnp.float32) / grid_y)
    lateral = 4.0 * wave_x[:, None] ** 2 + 4.0 * wave_y[None, :] ** 2
    ratios = []
    primes = []
    for layer_no in range(layers):
        diagonal = permittivity[layer_no] * lateral + interfaces[layer_no] + interfaces[layer_no + 1]
        source = spectrum[layer_no]
        if layer_no == 0:
            pivot_now = diagonal
            primed = source / pivot_now
        else:
            pivot_now = diagonal - interfaces[layer_no] * ratios[-1]
            primed = (source + interfaces[layer_no] * primes[-1]) / pivot_now
        primes.append(primed)
        ratios.append(interfaces[layer_no + 1] / pivot_now)
    values = [primes[-1]]
    for layer_no in range(layers - 2, -1, -1):
        values.insert(0, primes[layer_no] + ratios[layer_no] * values[0])
    potential = jnp.real(jnp.fft.ifft2(jnp.stack(values)))
    along_x = -0.5 * (jnp.roll(potential, -1, 1) - jnp.roll(potential, 1, 1))
    along_y = -0.5 * (jnp.roll(potential, -1, 2) - jnp.roll(potential, 1, 2))
    along_z = -0.5 * (shift_up(potential, 0) - shift_down(potential, 0))
    return jnp.stack([along_x, along_y, along_z])


def evolve(centre, alpha_field, landau, stiffness, field_now):
    squares = centre * centre
    total = squares[0] + squares[1] + squares[2]
    quartic = landau[0][None, :, None, None]
    mixed = landau[1][None, :, None, None]
    sextic = landau[2][None, :, None, None]
    kappa = stiffness[None, :, None, None]
    lateral = (jnp.roll(centre, -1, 2) + jnp.roll(centre, 1, 2) + jnp.roll(centre, -1, 3)
               + jnp.roll(centre, 1, 3) - 4.0 * centre)
    vertical = shift_up(centre, 1) + shift_down(centre, 1) - 2.0 * centre
    drive = (2.0 * alpha_field[None] * centre + 4.0 * quartic * centre * squares
             + 2.0 * mixed * centre * (total[None] - squares) + 6.0 * sextic * centre * squares * squares)
    smooth = kappa * (lateral + vertical)
    return centre - step_size * (drive - smooth - field_now)


def reference(polarization, alpha_field, landau, stiffness, permittivity, interfaces):
    polar_now = polarization
    field_now = jnp.zeros_like(polarization)
    for step_no in range(STEPS):
        field_now = depolarize(polar_now, permittivity, interfaces)
        polar_now = evolve(polar_now, alpha_field, landau, stiffness, field_now)
    return polar_now, field_now
```

```python
import functools

import jax
import jax.numpy as jnp
from jax import lax
from jax.experimental import pallas as pl
from jax.experimental.pallas import tpu as pltpu
from jax.sharding import PartitionSpec as P

STEPS = 2
step_size = 0.05
MESH = pl.DeviceIdType.MESH
PAD = 8


def cas_table(left, right, length):
    turns = left * right % length
    angle = 2.0 * jnp.pi / length * turns.astype(jnp.float32)
    table = jnp.cos(angle) + jnp.sin(angle)
    high = lax.reduce_precision(table, 8, 7)
    return jnp.stack([high.astype(jnp.bfloat16), (table - high).astype(jnp.bfloat16)])


def halves(value):
    high = value.astype(jnp.bfloat16)
    low = (value - high.astype(jnp.float32)).astype(jnp.bfloat16)
    return high, low


def product(left, right):
    dot = functools.partial(jnp.dot, preferred_element_type=jnp.float32)
    return dot(left[0], right[0]) + (dot(left[0], right[1]) + dot(left[1], right[0]))


def kernel(sizes, p_in, alpha, landau, stiff, perm, inter, lam, hx, hy, p_out, f_out, *scratch):
    L, R, C, nbx, nby, rep, lp, own = sizes
    (p_mid, base, coef, ratio, q, inb, outs, rec_f, rec_i, ybuf, phat, u,
     row_s, row_r, col_s, col_r, pc_s, pc_r, ssem, rsem) = scratch
    R2 = R + PAD
    bx = lax.axis_index("bx")
    by = lax.axis_index("by")
    group = bx // rep
    part = bx % rep
    scale = 1.0 / (R * nbx * C * nby)
    slots = [0]
    sends = []

    barrier = pltpu.get_barrier_semaphore()
    for k in range(1, nbx):
        pl.semaphore_signal(barrier, inc=1, device_id={"bx": (bx + k) % nbx}, device_id_type=MESH)
    for k in range(1, nby):
        pl.semaphore_signal(barrier, inc=1, device_id={"by": (by + k) % nby}, device_id_type=MESH)

    def remote(src, dst, device, slot):
        return pltpu.make_async_remote_copy(
            src_ref=src, dst_ref=dst, send_sem=ssem.at[slot], recv_sem=rsem.at[slot],
            device_id=device, device_id_type=MESH)

    def fresh():
        slots[0] += 1
        return slots[0] - 1

    def push(src, dst, device):
        copy = remote(src, dst, device, fresh())
        copy.start()
        sends.append(copy.wait_send)
        return copy

    rows = lax.broadcasted_iota(jnp.int32, (R, C), 0)
    lanes = lax.broadcasted_iota(jnp.int32, (R, C), 1)

    def x_next(f, high):
        return jnp.where(rows == R - 1, high, pltpu.roll(f, R - 1, 0))

    def x_prev(f, low):
        return jnp.where(rows == 0, low, pltpu.roll(f, 1, 0))

    def y_next(f, high):
        return jnp.where(lanes == C - 1, high, pltpu.roll(f, C - 1, 1))

    def y_prev(f, low):
        return jnp.where(lanes == 0, low, pltpu.roll(f, 1, 1))

    def column_tile(blocks):
        tile = jnp.zeros((R, C), jnp.float32)
        for at, block in enumerate(blocks):
            tile = jnp.where(lanes == at, block[:, 0:1], tile)
            tile = jnp.where(lanes == C // 2 + at, block[:, C - 1:C], tile)
        return tile

    def x_start(src, n):
        mine = inb.at[n, :, pl.ds(pl.multiple_of(bx * R, R), R)]
        copies = []
        for k in range(1, nbx):
            to = (bx + k) % nbx
            copies.append(push(src.at[pl.ds(to // rep * lp, lp)], mine, {"bx": to}))
        for layer in range(lp):
            inb[n, layer, pl.ds(pl.multiple_of(bx * R, R), R)] = src[group * lp + layer]
        return copies

    def x_finish(copies, n, dst, height):
        for copy in copies:
            copy.wait_recv()
        table = (hx[0], hx[1])
        for layer in range(lp):
            outs[n, :, layer] = product(table, halves(inb[n, layer])).reshape(own, R2, C)
        waits = []
        landing = dst.at[pl.ds(group * lp, lp)]
        for t in range(own):
            local = (group + t) % own
            to = part * own + local
            src = outs.at[n, local, :, pl.ds(0, height)]
            if rep == 1:
                if t == 0:
                    continue
                waits.append(push(src, landing, {"bx": to}).wait_recv)
                continue
            slot = fresh()

            def go(src=src, to=to, slot=slot):
                remote(src, landing, {"bx": to}, slot).start()

            def gone(src=src, to=to, slot=slot):
                @pl.when(to != bx)
                def _():
                    remote(src, landing, {"bx": to}, slot).wait_send()

            def came(src=src, to=to, slot=slot, t=t):
                origin = (bx % own + own - t) % own * rep + bx // own

                @pl.when(origin != bx)
                def _():
                    remote(src, landing, {"bx": to}, slot).wait_recv()

            pl.when(to != bx)(go)
            sends.append(gone)
            waits.append(came)

        def keep():
            for layer in range(lp):
                dst[group * lp + layer] = outs[n, bx % own, layer, 0:height]

        if rep == 1:
            keep()
        else:
            pl.when(bx // own == part)(keep)
        for wait in waits:
            wait()

    def y_pass(src, n):
        copies = [push(src, ybuf.at[n, k - 1], {"by": (by + k) % nby}) for k in range(1, nby)]
        total = product(halves(src[...].reshape(L * R, C)), (hy[0, by], hy[1, by]))
        for k in range(1, nby):
            copies[k - 1].wait_recv()
            origin = (by + nby - k) % nby
            total += product(halves(ybuf[n, k - 1].reshape(L * R, C)), (hy[0, origin], hy[1, origin]))
        return total

    def flank_start(rows_too, step, src):
        copies = []
        if rows_too:
            for c in range(3):
                for l in range(L):
                    at = c * L + l
                    row_s[step, 0, at:at + 1] = src[c, l, 0:1]
                    row_s[step, 1, at:at + 1] = src[c, l, R - 1:R]
            col_s[step] = column_tile([src[c, l] for c in range(3) for l in range(L)])
            if step == 0:
                pl.semaphore_wait(barrier, nbx + nby - 2)
            copies.append(push(row_s.at[step, 1], row_r.at[step, 0], {"bx": (bx + 1) % nbx}))
            copies.append(push(row_s.at[step, 0], row_r.at[step, 1], {"bx": (bx + nbx - 1) % nbx}))
            tile, land = col_s.at[step], col_r
        else:
            pc_s[step] = column_tile([src[l, 0:R] for l in range(L)])
            tile, land = pc_s.at[step], pc_r
        copies.append(push(tile, land.at[step, 0], {"by": (by + 1) % nby}))
        copies.append(push(tile, land.at[step, 1], {"by": (by + nby - 1) % nby}))
        return copies

    for step in range(STEPS):
        src = p_in if step == 0 else p_mid
        flanks = flank_start(True, step, src)
        if step == 0:
            lateral = lam[...]
            previous = None
            for l in range(L):
                pivot = perm[l] * lateral + inter[l] + inter[l + 1]
                if l:
                    pivot = pivot - inter[l] * previous
                inverse = 1.0 / pivot
                coef[l] = inverse
                previous = inter[l + 1] * inverse
                ratio[l] = previous
        for copy in flanks:
            copy.wait_recv()
        low_col = col_r[step, 0]
        high_col = col_r[step, 1]

        def edges(c, l):
            at = c * L + l
            return (row_r[step, 0, at:at + 1], row_r[step, 1, at:at + 1],
                    low_col[:, C // 2 + at:C // 2 + at + 1], high_col[:, at:at + 1])

        zero = jnp.zeros((R, C), jnp.float32)
        for l in range(L):
            low, high, _, _ = edges(0, l)
            _, _, left, right = edges(1, l)
            along_x, along_y = src[0, l], src[1, l]
            above = src[2, l + 1] if l + 1 < L else zero
            below = src[2, l - 1] if l else zero
            q[step, l] = -0.5 * (
                (x_next(along_x, high) - x_prev(along_x, low))
                + (y_next(along_y, right) - y_prev(along_y, left)) + (above - below))
        copies = x_start(q.at[step], 2 * step)
        for l in range(L):
            cells = [src[c, l] for c in range(3)]
            squares = [cell * cell for cell in cells]
            whole = squares[0] + squares[1] + squares[2]
            for c in range(3):
                cell, square = cells[c], squares[c]
                low, high, left, right = edges(c, l)
                above = src[c, l + 1] if l + 1 < L else zero
                below = src[c, l - 1] if l else zero
                smooth = stiff[l] * (
                    (x_next(cell, high) + x_prev(cell, low) + y_next(cell, right)
                     + y_prev(cell, left) - 4.0 * cell) + (above + below - 2.0 * cell))
                drive = cell * (
                    2.0 * alpha[l] + 4.0 * landau[0, l] * square
                    + 2.0 * landau[1, l] * (whole - square)
                    + 6.0 * landau[2, l] * (square * square))
                base[c, l] = cell - step_size * (drive - smooth)
        x_finish(copies, 2 * step, rec_f.at[step], R)
        spectrum = y_pass(rec_f.at[step], 2 * step)
        primes = []
        for l in range(L):
            source = spectrum[l * R:(l + 1) * R] * scale
            if l:
                source = source + inter[l] * primes[-1]
            primes.append(source * coef[l])
        value = primes[-1]
        phat[step, L - 1] = value
        for l in range(L - 2, -1, -1):
            value = primes[l] + ratio[l] * value
            phat[step, l] = value
        u[step] = y_pass(phat.at[step], 2 * step + 1).reshape(L, R, C)
        x_finish(x_start(u.at[step], 2 * step + 1), 2 * step + 1, rec_i.at[step], R2)
        flanks = flank_start(False, step, rec_i.at[step])
        last = step == STEPS - 1
        target = p_out if last else p_mid
        for l in range(L):
            phi = rec_i[step, l, 0:R]
            low = rec_i[step, l, R:R + 1]
            high = rec_i[step, l, R + 1:R + 2]
            along_x = -0.5 * (x_next(phi, high) - x_prev(phi, low))
            above = rec_i[step, l + 1, 0:R] if l + 1 < L else zero
            below = rec_i[step, l - 1, 0:R] if l else zero
            along_z = -0.5 * (above - below)
            target[0, l] = base[0, l] + step_size * along_x
            target[2, l] = base[2, l] + step_size * along_z
            if last:
                f_out[0, l] = along_x
                f_out[2, l] = along_z
        for copy in flanks:
            copy.wait_recv()
        low_phi = pc_r[step, 0]
        high_phi = pc_r[step, 1]
        for l in range(L):
            phi = rec_i[step, l, 0:R]
            along_y = -0.5 * (y_next(phi, high_phi[:, l:l + 1])
                              - y_prev(phi, low_phi[:, C // 2 + l:C // 2 + l + 1]))
            target[1, l] = base[1, l] + step_size * along_y
            if last:
                f_out[1, l] = along_y
    for wait in sends:
        wait()


def shards(polarization, alpha_field, landau, stiffness, permittivity, interfaces):
    _, L, R, C = polarization.shape
    nbx = lax.axis_size("bx")
    nby = lax.axis_size("by")
    bx = lax.axis_index("bx")
    by = lax.axis_index("by")
    rep = max(1, nbx // L)
    lp = max(1, L // nbx)
    own = nbx // rep
    grid_x, grid_y = nbx * R, nby * C
    R2 = R + PAD
    line = jnp.arange(R2, dtype=jnp.int32)
    line = jnp.where(line < R, line, jnp.where(line == R, -1, R))
    owners = bx % rep * own + jnp.arange(own, dtype=jnp.int32)
    wanted = ((owners[:, None] * R + line[None, :] + grid_x) % grid_x).reshape(own * R2, 1)
    hx = cas_table(wanted, jnp.arange(grid_x, dtype=jnp.int32)[None, :], grid_x)
    my_cols = by * C + jnp.arange(C, dtype=jnp.int32)
    hy = cas_table(jnp.arange(grid_y, dtype=jnp.int32)[:, None], my_cols[None, :], grid_y)
    hy = hy.reshape(2, nby, C, C)
    my_rows = bx * R + jnp.arange(R, dtype=jnp.int32)
    wave_x = jnp.sin(jnp.pi * my_rows.astype(jnp.float32) / grid_x)
    wave_y = jnp.sin(jnp.pi * my_cols.astype(jnp.float32) / grid_y)
    lam = 4.0 * wave_x[:, None] ** 2 + 4.0 * wave_y[None, :] ** 2
    sizes = (L, R, C, nbx, nby, rep, lp, own)
    n_copies = STEPS * (6 + 2 * (nbx - 1 + own + nby - 1))
    f32 = jnp.float32
    vmem = pl.BlockSpec(memory_space=pltpu.VMEM)
    smem = pl.BlockSpec(memory_space=pltpu.SMEM)
    S = STEPS
    scratch = [
        pltpu.VMEM((3, L, R, C), f32), pltpu.VMEM((3, L, R, C), f32),
        pltpu.VMEM((L, R, C), f32), pltpu.VMEM((L, R, C), f32),
        pltpu.VMEM((S, L, R, C), f32), pltpu.VMEM((2 * S, lp, grid_x, C), f32),
        pltpu.VMEM((2 * S, own, lp, R2, C), f32), pltpu.VMEM((S, L, R, C), f32),
        pltpu.VMEM((S, L, R2, C), f32), pltpu.VMEM((2 * S, nby - 1, L, R, C), f32),
        pltpu.VMEM((S, L, R, C), f32), pltpu.VMEM((S, L, R, C), f32),
        pltpu.VMEM((S, 2, 3 * L, C), f32), pltpu.VMEM((S, 2, 3 * L, C), f32),
        pltpu.VMEM((S, R, C), f32), pltpu.VMEM((S, 2, R, C), f32),
        pltpu.VMEM((S, R, C), f32), pltpu.VMEM((S, 2, R, C), f32),
        pltpu.SemaphoreType.DMA((n_copies,)), pltpu.SemaphoreType.DMA((n_copies,)),
    ]
    out = jax.ShapeDtypeStruct(polarization.shape, f32)
    return pl.pallas_call(
        functools.partial(kernel, sizes),
        out_shape=(out, out),
        in_specs=[vmem, vmem, smem, smem, smem, smem, vmem, vmem, vmem],
        out_specs=(vmem, vmem),
        scratch_shapes=scratch,
        compiler_params=pltpu.CompilerParams(
            collective_id=0, has_side_effects=True, vmem_limit_bytes=48 * 1024 * 1024),
    )(polarization, alpha_field, landau, stiffness, permittivity, interfaces, lam, hx, hy)


def solution(mesh):
    return jax.shard_map(
        shards,
        mesh=mesh,
        in_specs=(P(None, None, "bx", "by"), P(None, "bx", "by"), P(), P(), P(), P()),
        out_specs=(P(None, None, "bx", "by"), P(None, None, "bx", "by")),
        check_vma=False,
    )
```

```python
import functools

import jax
import jax.numpy as jnp
import numpy as np
from jax import lax
from jax.experimental import pallas as pl
from jax.experimental.pallas import tpu as pltpu
from jax.sharding import PartitionSpec as P

STEPS = 2
step_size = 0.05
MESH = pl.DeviceIdType.MESH
PAD = 8


def cas_table(left, right, length):
    turns = left * right % length
    angle = 2.0 * jnp.pi / length * turns.astype(jnp.float32)
    table = jnp.cos(angle) + jnp.sin(angle)
    high = lax.reduce_precision(table, 8, 7)
    return jnp.stack([high.astype(jnp.bfloat16), (table - high).astype(jnp.bfloat16)])


def fixed_table(left, right, length):
    angle = 2.0 * np.pi / length * (left * right % length)
    table = (np.cos(angle) + np.sin(angle)).astype(np.float32)
    high = table.astype(jnp.bfloat16)
    low = (table - high.astype(np.float32)).astype(jnp.bfloat16)
    return jnp.asarray(np.stack([high, low]))


def is_wide(rows, nbx, nby, layers):
    return layers % nbx == 0 and rows % (8 * nby) == 0


def halves(value):
    high = value.astype(jnp.bfloat16)
    low = (value - high.astype(jnp.float32)).astype(jnp.bfloat16)
    return high, low


def product(left, right):
    dot = functools.partial(jnp.dot, preferred_element_type=jnp.float32)
    return dot(left[0], right[0]) + (dot(left[0], right[1]) + dot(left[1], right[0]))


def kernel(sizes, p_in, alpha, landau, stiff, perm, inter, lam, hx, hy, p_out, f_out, *scratch):
    L, R, C, nbx, nby, rep, lp, own = sizes
    (p_mid, base, coef, ratio, q, inb, outs, rec_i,
     row_s, row_r, col_s, col_r, pc_s, pc_r, ssem, rsem) = scratch[:16]
    wide = is_wide(R, nbx, nby, L)
    if wide:
        z_in, w_out = scratch[16:]
    else:
        rec_f, ybuf, phat, u = scratch[16:]
    thin = R // nby
    R2 = R + PAD
    bx = lax.axis_index("bx")
    by = lax.axis_index("by")
    group = bx // rep
    part = bx % rep
    scale = 1.0 / (R * nbx * C * nby)
    slots = [0]
    sends = []

    barrier = pltpu.get_barrier_semaphore()
    others = [(a, b) for b in range(nby) for a in range(nbx) if a or b]
    greeted = [(a, b) for a, b in others if wide or not a or not b]
    for a, b in greeted:
        pl.semaphore_signal(
            barrier, inc=1, device_id={"bx": (bx + a) % nbx, "by": (by + b) % nby},
            device_id_type=MESH)

    def remote(src, dst, device, slot):
        return pltpu.make_async_remote_copy(
            src_ref=src, dst_ref=dst, send_sem=ssem.at[slot], recv_sem=rsem.at[slot],
            device_id=device, device_id_type=MESH)

    def fresh():
        slots[0] += 1
        return slots[0] - 1

    def push(src, dst, device):
        copy = remote(src, dst, device, fresh())
        copy.start()
        sends.append(copy.wait_send)
        return copy

    rows = lax.broadcasted_iota(jnp.int32, (R, C), 0)
    lanes = lax.broadcasted_iota(jnp.int32, (R, C), 1)

    def x_next(f, high):
        return jnp.where(rows == R - 1, high, pltpu.roll(f, R - 1, 0))

    def x_prev(f, low):
        return jnp.where(rows == 0, low, pltpu.roll(f, 1, 0))

    def y_next(f, high):
        return jnp.where(lanes == C - 1, high, pltpu.roll(f, C - 1, 1))

    def y_prev(f, low):
        return jnp.where(lanes == 0, low, pltpu.roll(f, 1, 1))

    def column_tile(blocks):
        tile = jnp.zeros((R, C), jnp.float32)
        for at, block in enumerate(blocks):
            tile = jnp.where(lanes == at, block[:, 0:1], tile)
            tile = jnp.where(lanes == C // 2 + at, block[:, C - 1:C], tile)
        return tile

    def x_start(src, n):
        mine = inb.at[n, :, pl.ds(pl.multiple_of(bx * R, R), R)]
        copies = []
        for k in range(1, nbx):
            to = (bx + k) % nbx
            copies.append(push(src.at[pl.ds(to // rep * lp, lp)], mine, {"bx": to}))
        for layer in range(lp):
            inb[n, layer, pl.ds(pl.multiple_of(bx * R, R), R)] = src[group * lp + layer]
        return copies

    def x_mix(copies, n):
        for copy in copies:
            copy.wait_recv()
        table = (hx[0], hx[1])
        for layer in range(lp):
            outs[n, :, layer] = product(table, halves(inb[n, layer])).reshape(own, R2, C)

    def spread(n, step):
        copies = []
        for a, b in others:
            to_x, to_y = (bx + a) % nbx, (by + b) % nby
            copies.append(push(
                outs.at[n, to_x, :, pl.ds(pl.multiple_of(to_y * thin, thin), thin)],
                z_in.at[step, by, pl.ds(bx * lp, lp)], {"bx": to_x, "by": to_y}))
        for layer in range(lp):
            z_in[step, by, bx * lp + layer] = outs[
                n, bx, layer, pl.ds(pl.multiple_of(by * thin, thin), thin)]
        for copy in copies:
            copy.wait_recv()

    def collect(n, step):
        at = pl.ds(pl.multiple_of(bx * R + by * thin, thin), thin)
        copies = []
        for a, b in others:
            to_x, to_y = (bx + a) % nbx, (by + b) % nby
            copies.append(push(
                w_out.at[step, to_y, pl.ds(to_x * lp, lp)], inb.at[n, :, at],
                {"bx": to_x, "by": to_y}))
        for layer in range(lp):
            inb[n, layer, at] = w_out[step, by, bx * lp + layer]
        return copies

    def solve(spectrum, height):
        primes = []
        for l in range(L):
            source = spectrum[l * height:(l + 1) * height] * scale
            if l:
                source = source + inter[l] * primes[-1]
            primes.append(source * coef[l])
        values = [primes[-1]]
        for l in range(L - 2, -1, -1):
            values.insert(0, primes[l] + ratio[l] * values[0])
        return values

    def x_finish(n, dst, height):
        waits = []
        landing = dst.at[pl.ds(group * lp, lp)]
        for t in range(own):
            local = (group + t) % own
            to = part * own + local
            src = outs.at[n, local, :, pl.ds(0, height)]
            if rep == 1:
                if t == 0:
                    continue
                waits.append(push(src, landing, {"bx": to}).wait_recv)
                continue
            slot = fresh()

            def go(src=src, to=to, slot=slot):
                remote(src, landing, {"bx": to}, slot).start()

            def gone(src=src, to=to, slot=slot):
                @pl.when(to != bx)
                def _():
                    remote(src, landing, {"bx": to}, slot).wait_send()

            def came(src=src, to=to, slot=slot, t=t):
                origin = (bx % own + own - t) % own * rep + bx // own

                @pl.when(origin != bx)
                def _():
                    remote(src, landing, {"bx": to}, slot).wait_recv()

            pl.when(to != bx)(go)
            sends.append(gone)
            waits.append(came)

        def keep():
            for layer in range(lp):
                dst[group * lp + layer] = outs[n, bx % own, layer, 0:height]

        if rep == 1:
            keep()
        else:
            pl.when(bx // own == part)(keep)
        for wait in waits:
            wait()

    def y_pass(src, n):
        copies = [push(src, ybuf.at[n, k - 1], {"by": (by + k) % nby}) for k in range(1, nby)]
        total = product(halves(src[...].reshape(L * R, C)), (hy[0, by], hy[1, by]))
        for k in range(1, nby):
            copies[k - 1].wait_recv()
            origin = (by + nby - k) % nby
            total += product(halves(ybuf[n, k - 1].reshape(L * R, C)), (hy[0, origin], hy[1, origin]))
        return total

    def flank_start(rows_too, step, src):
        copies = []
        if rows_too:
            for c in range(3):
                for l in range(L):
                    at = c * L + l
                    row_s[step, 0, at:at + 1] = src[c, l, 0:1]
                    row_s[step, 1, at:at + 1] = src[c, l, R - 1:R]
            col_s[step] = column_tile([src[c, l] for c in range(3) for l in range(L)])
            if step == 0:
                pl.semaphore_wait(barrier, len(greeted))
            copies.append(push(row_s.at[step, 1], row_r.at[step, 0], {"bx": (bx + 1) % nbx}))
            copies.append(push(row_s.at[step, 0], row_r.at[step, 1], {"bx": (bx + nbx - 1) % nbx}))
            tile, land = col_s.at[step], col_r
        else:
            pc_s[step] = column_tile([src[l, 0:R] for l in range(L)])
            tile, land = pc_s.at[step], pc_r
        copies.append(push(tile, land.at[step, 0], {"by": (by + 1) % nby}))
        copies.append(push(tile, land.at[step, 1], {"by": (by + nby - 1) % nby}))
        return copies

    for step in range(STEPS):
        src = p_in if step == 0 else p_mid
        flanks = flank_start(True, step, src)
        if step == 0:
            lateral = lam[...]
            previous = None
            for l in range(L):
                pivot = perm[l] * lateral + inter[l] + inter[l + 1]
                if l:
                    pivot = pivot - inter[l] * previous
                inverse = 1.0 / pivot
                coef[l] = inverse
                previous = inter[l + 1] * inverse
                ratio[l] = previous
        for copy in flanks:
            copy.wait_recv()
        low_col = col_r[step, 0]
        high_col = col_r[step, 1]

        def edges(c, l):
            at = c * L + l
            return (row_r[step, 0, at:at + 1], row_r[step, 1, at:at + 1],
                    low_col[:, C // 2 + at:C // 2 + at + 1], high_col[:, at:at + 1])

        zero = jnp.zeros((R, C), jnp.float32)
        for l in range(L):
            low, high, _, _ = edges(0, l)
            _, _, left, right = edges(1, l)
            along_x, along_y = src[0, l], src[1, l]
            above = src[2, l + 1] if l + 1 < L else zero
            below = src[2, l - 1] if l else zero
            q[step, l] = -0.5 * (
                (x_next(along_x, high) - x_prev(along_x, low))
                + (y_next(along_y, right) - y_prev(along_y, left)) + (above - below))
        copies = x_start(q.at[step], 2 * step)
        for l in range(L):
            cells = [src[c, l] for c in range(3)]
            squares = [cell * cell for cell in cells]
            whole = squares[0] + squares[1] + squares[2]
            for c in range(3):
                cell, square = cells[c], squares[c]
                low, high, left, right = edges(c, l)
                above = src[c, l + 1] if l + 1 < L else zero
                below = src[c, l - 1] if l else zero
                smooth = stiff[l] * (
                    (x_next(cell, high) + x_prev(cell, low) + y_next(cell, right)
                     + y_prev(cell, left) - 4.0 * cell) + (above + below - 2.0 * cell))
                drive = cell * (
                    2.0 * alpha[l] + 4.0 * landau[0, l] * square
                    + 2.0 * landau[1, l] * (whole - square)
                    + 6.0 * landau[2, l] * (square * square))
                base[c, l] = cell - step_size * (drive - smooth)
        n = 2 * step
        x_mix(copies, n)
        if wide:
            spread(n, step)
            table = (hy[0], hy[1])
            full = jnp.concatenate(
                [z_in[step, j].reshape(L * thin, C) for j in range(nby)], axis=1)
            values = solve(product(halves(full), table), thin)
            full = product(halves(jnp.concatenate(values, axis=0)), table)
            for j in range(nby):
                w_out[step, j] = full[:, j * C:(j + 1) * C].reshape(L, thin, C)
            copies = collect(n + 1, step)
        else:
            x_finish(n, rec_f.at[step], R)
            for l, value in enumerate(solve(y_pass(rec_f.at[step], n), R)):
                phat[step, l] = value
            u[step] = y_pass(phat.at[step], n + 1).reshape(L, R, C)
            copies = x_start(u.at[step], n + 1)
        x_mix(copies, n + 1)
        x_finish(n + 1, rec_i.at[step], R2)
        flanks = flank_start(False, step, rec_i.at[step])
        last = step == STEPS - 1
        target = p_out if last else p_mid
        for l in range(L):
            phi = rec_i[step, l, 0:R]
            low = rec_i[step, l, R:R + 1]
            high = rec_i[step, l, R + 1:R + 2]
            along_x = -0.5 * (x_next(phi, high) - x_prev(phi, low))
            above = rec_i[step, l + 1, 0:R] if l + 1 < L else zero
            below = rec_i[step, l - 1, 0:R] if l else zero
            along_z = -0.5 * (above - below)
            target[0, l] = base[0, l] + step_size * along_x
            target[2, l] = base[2, l] + step_size * along_z
            if last:
                f_out[0, l] = along_x
                f_out[2, l] = along_z
        for copy in flanks:
            copy.wait_recv()
        low_phi = pc_r[step, 0]
        high_phi = pc_r[step, 1]
        for l in range(L):
            phi = rec_i[step, l, 0:R]
            along_y = -0.5 * (y_next(phi, high_phi[:, l:l + 1])
                              - y_prev(phi, low_phi[:, C // 2 + l:C // 2 + l + 1]))
            target[1, l] = base[1, l] + step_size * along_y
            if last:
                f_out[1, l] = along_y
    for wait in sends:
        wait()


def shards(polarization, alpha_field, landau, stiffness, permittivity, interfaces):
    _, L, R, C = polarization.shape
    nbx = lax.axis_size("bx")
    nby = lax.axis_size("by")
    bx = lax.axis_index("bx")
    by = lax.axis_index("by")
    rep = max(1, nbx // L)
    lp = max(1, L // nbx)
    own = nbx // rep
    grid_x, grid_y = nbx * R, nby * C
    R2 = R + PAD
    wide = is_wide(R, nbx, nby, L)
    pool = np if wide else jnp
    make = fixed_table if wide else cas_table
    line = pool.arange(R2, dtype=jnp.int32)
    line = pool.where(line < R, line, pool.where(line == R, -1, R))
    owners = pool.arange(own, dtype=jnp.int32)
    if not wide:
        owners = owners + bx % rep * own
    wanted = ((owners[:, None] * R + line[None, :] + grid_x) % grid_x).reshape(own * R2, 1)
    hx = make(wanted, pool.arange(grid_x, dtype=jnp.int32)[None, :], grid_x)
    every_col = pool.arange(grid_y, dtype=jnp.int32)
    my_rows = bx * R + jnp.arange(R, dtype=jnp.int32)
    my_cols = by * C + jnp.arange(C, dtype=jnp.int32)
    if wide:
        hy = make(every_col[:, None], every_col[None, :], grid_y)
        my_rows = bx * R + by * (R // nby) + jnp.arange(R // nby, dtype=jnp.int32)
        my_cols = jnp.arange(grid_y, dtype=jnp.int32)
    else:
        hy = make(every_col[:, None], my_cols[None, :], grid_y).reshape(2, nby, C, C)
    wave_x = jnp.sin(jnp.pi * my_rows.astype(jnp.float32) / grid_x)
    wave_y = jnp.sin(jnp.pi * my_cols.astype(jnp.float32) / grid_y)
    lam = 4.0 * wave_x[:, None] ** 2 + 4.0 * wave_y[None, :] ** 2
    sizes = (L, R, C, nbx, nby, rep, lp, own)
    n_copies = STEPS * (6 + 2 * (nbx * nby + own if wide else nbx + own + nby))
    f32 = jnp.float32
    vmem = pl.BlockSpec(memory_space=pltpu.VMEM)
    smem = pl.BlockSpec(memory_space=pltpu.SMEM)
    S = STEPS
    scratch = [
        pltpu.VMEM((3, L, R, C), f32), pltpu.VMEM((3, L, R, C), f32),
        pltpu.VMEM((L,) + lam.shape, f32), pltpu.VMEM((L,) + lam.shape, f32),
        pltpu.VMEM((S, L, R, C), f32), pltpu.VMEM((2 * S, lp, grid_x, C), f32),
        pltpu.VMEM((2 * S, own, lp, R2, C), f32), pltpu.VMEM((S, L, R2, C), f32),
        pltpu.VMEM((S, 2, 3 * L, C), f32), pltpu.VMEM((S, 2, 3 * L, C), f32),
        pltpu.VMEM((S, R, C), f32), pltpu.VMEM((S, 2, R, C), f32),
        pltpu.VMEM((S, R, C), f32), pltpu.VMEM((S, 2, R, C), f32),
        pltpu.SemaphoreType.DMA((n_copies,)), pltpu.SemaphoreType.DMA((n_copies,)),
    ]
    if wide:
        thin = (S, nby, L, R // nby, C)
        scratch += [pltpu.VMEM(thin, f32), pltpu.VMEM(thin, f32)]
    else:
        scratch += [
            pltpu.VMEM((S, L, R, C), f32), pltpu.VMEM((2 * S, nby - 1, L, R, C), f32),
            pltpu.VMEM((S, L, R, C), f32), pltpu.VMEM((S, L, R, C), f32),
        ]
    out = jax.ShapeDtypeStruct(polarization.shape, f32)
    return pl.pallas_call(
        functools.partial(kernel, sizes),
        out_shape=(out, out),
        in_specs=[vmem, vmem, smem, smem, smem, smem, vmem, vmem, vmem],
        out_specs=(vmem, vmem),
        scratch_shapes=scratch,
        compiler_params=pltpu.CompilerParams(
            collective_id=0, has_side_effects=True, vmem_limit_bytes=48 * 1024 * 1024),
    )(polarization, alpha_field, landau, stiffness, permittivity, interfaces, lam, hx, hy)


def solution(mesh):
    return jax.shard_map(
        shards,
        mesh=mesh,
        in_specs=(P(None, None, "bx", "by"), P(None, "bx", "by"), P(), P(), P(), P()),
        out_specs=(P(None, None, "bx", "by"), P(None, None, "bx", "by")),
        check_vma=False,
    )
```

```python
import functools

import jax
import jax.numpy as jnp
import numpy as np
from jax import lax
from jax.experimental import pallas as pl
from jax.experimental.pallas import tpu as pltpu
from jax.sharding import PartitionSpec as P

STEPS = 2
step_size = 0.05
MESH = pl.DeviceIdType.MESH


def cas_table(left, right, length):
    turns = left * right % length
    angle = 2.0 * jnp.pi / length * turns.astype(jnp.float32)
    table = jnp.cos(angle) + jnp.sin(angle)
    high = lax.reduce_precision(table, 8, 7)
    return jnp.stack([high.astype(jnp.bfloat16), (table - high).astype(jnp.bfloat16)])


def fixed_table(left, right, length):
    angle = 2.0 * np.pi / length * (left * right % length)
    table = (np.cos(angle) + np.sin(angle)).astype(np.float32)
    high = table.astype(jnp.bfloat16)
    low = (table - high.astype(np.float32)).astype(jnp.bfloat16)
    return jnp.asarray(np.stack([high, low]))


def is_wide(rows, nbx, nby, layers):
    return layers % nbx == 0 and rows % (8 * nby) == 0


def halves(value):
    high = value.astype(jnp.bfloat16)
    low = (value - high.astype(jnp.float32)).astype(jnp.bfloat16)
    return high, low


def product(left, right):
    dot = functools.partial(jnp.dot, preferred_element_type=jnp.float32)
    return dot(left[0], right[0]) + (dot(left[0], right[1]) + dot(left[1], right[0]))


def kernel(sizes, p_in, alpha_h, landau, stiff, perm, inter, lam, hx_h, hy_h, p_out, f_out, *scratch):
    L, R, C, nbx, nby, rep, lp, own = sizes
    (p_mid, base, coef, ratio, q, inb, outs, rec_i,
     row_s, row_r, col_s, col_r, pr_s, pr_r, pc_s, pc_r, ssem, rsem,
     alpha, hx, hy, local_sem) = scratch[:22]
    wide = is_wide(R, nbx, nby, L)
    if wide:
        z_in, w_out = scratch[22:]
    else:
        rec_f, ybuf, phat, u = scratch[22:]
    thin = R // nby
    bx = lax.axis_index("bx")
    by = lax.axis_index("by")
    group = bx // rep
    part = bx % rep
    scale = 1.0 / (R * nbx * C * nby)
    loads = [pltpu.make_async_copy(src, dst, local_sem.at[at]) for at, (src, dst) in
             enumerate(((alpha_h, alpha), (hx_h, hx), (hy_h, hy)))]
    for load in loads:
        load.start()
    slots = [0]
    sends = []

    barrier = pltpu.get_barrier_semaphore()
    others = [(a, b) for b in range(nby) for a in range(nbx) if a or b]
    greeted = [(a, b) for a, b in others if wide or not a or not b]
    for a, b in greeted:
        pl.semaphore_signal(
            barrier, inc=1, device_id={"bx": (bx + a) % nbx, "by": (by + b) % nby},
            device_id_type=MESH)

    def remote(src, dst, device, slot):
        return pltpu.make_async_remote_copy(
            src_ref=src, dst_ref=dst, send_sem=ssem.at[slot], recv_sem=rsem.at[slot],
            device_id=device, device_id_type=MESH)

    def fresh():
        slots[0] += 1
        return slots[0] - 1

    def push(src, dst, device):
        copy = remote(src, dst, device, fresh())
        copy.start()
        sends.append(copy.wait_send)
        return copy

    rows = lax.broadcasted_iota(jnp.int32, (R, C), 0)
    lanes = lax.broadcasted_iota(jnp.int32, (R, C), 1)

    def x_next(f, high):
        return jnp.where(rows == R - 1, high, pltpu.roll(f, R - 1, 0))

    def x_prev(f, low):
        return jnp.where(rows == 0, low, pltpu.roll(f, 1, 0))

    def y_next(f, high):
        return jnp.where(lanes == C - 1, high, pltpu.roll(f, C - 1, 1))

    def y_prev(f, low):
        return jnp.where(lanes == 0, low, pltpu.roll(f, 1, 1))

    def column_tile(blocks):
        tile = jnp.zeros((R, C), jnp.float32)
        for at, block in enumerate(blocks):
            tile = jnp.where(lanes == at, block[:, 0:1], tile)
            tile = jnp.where(lanes == C // 2 + at, block[:, C - 1:C], tile)
        return tile

    def x_start(src, n):
        mine = inb.at[n, :, pl.ds(pl.multiple_of(bx * R, R), R)]
        copies = []
        for k in range(1, nbx):
            to = (bx + k) % nbx
            copies.append(push(src.at[pl.ds(to // rep * lp, lp)], mine, {"bx": to}))
        for layer in range(lp):
            inb[n, layer, pl.ds(pl.multiple_of(bx * R, R), R)] = src[group * lp + layer]
        return copies

    def x_mix(copies, n):
        for copy in copies:
            copy.wait_recv()
        table = (hx[0], hx[1])
        for layer in range(lp):
            outs[n, :, layer] = product(table, halves(inb[n, layer])).reshape(own, R, C)

    def spread(n, step):
        copies = []
        for a, b in others:
            to_x, to_y = (bx + a) % nbx, (by + b) % nby
            copies.append(push(
                outs.at[n, to_x, :, pl.ds(pl.multiple_of(to_y * thin, thin), thin)],
                z_in.at[step, by, pl.ds(bx * lp, lp)], {"bx": to_x, "by": to_y}))
        for layer in range(lp):
            z_in[step, by, bx * lp + layer] = outs[
                n, bx, layer, pl.ds(pl.multiple_of(by * thin, thin), thin)]
        for copy in copies:
            copy.wait_recv()

    def collect(n, step):
        at = pl.ds(pl.multiple_of(bx * R + by * thin, thin), thin)
        copies = []
        for a, b in others:
            to_x, to_y = (bx + a) % nbx, (by + b) % nby
            copies.append(push(
                w_out.at[step, to_y, pl.ds(to_x * lp, lp)], inb.at[n, :, at],
                {"bx": to_x, "by": to_y}))
        for layer in range(lp):
            inb[n, layer, at] = w_out[step, by, bx * lp + layer]
        return copies

    def solve(spectrum, height):
        primes = []
        for l in range(L):
            source = spectrum[l * height:(l + 1) * height] * scale
            if l:
                source = source + inter[l] * primes[-1]
            primes.append(source * coef[l])
        values = [primes[-1]]
        for l in range(L - 2, -1, -1):
            values.insert(0, primes[l] + ratio[l] * values[0])
        return values

    def x_finish(n, dst):
        waits = []
        landing = dst.at[pl.ds(group * lp, lp)]
        for t in range(own):
            local = (group + t) % own
            to = part * own + local
            src = outs.at[n, local]
            if rep == 1:
                if t == 0:
                    continue
                waits.append(push(src, landing, {"bx": to}).wait_recv)
                continue
            slot = fresh()

            def go(src=src, to=to, slot=slot):
                remote(src, landing, {"bx": to}, slot).start()

            def gone(src=src, to=to, slot=slot):
                @pl.when(to != bx)
                def _():
                    remote(src, landing, {"bx": to}, slot).wait_send()

            def came(src=src, to=to, slot=slot, t=t):
                origin = (bx % own + own - t) % own * rep + bx // own

                @pl.when(origin != bx)
                def _():
                    remote(src, landing, {"bx": to}, slot).wait_recv()

            pl.when(to != bx)(go)
            sends.append(gone)
            waits.append(came)

        def keep():
            for layer in range(lp):
                dst[group * lp + layer] = outs[n, bx % own, layer]

        if rep == 1:
            keep()
        else:
            pl.when(bx // own == part)(keep)
        for wait in waits:
            wait()

    def y_pass(src, n):
        copies = [push(src, ybuf.at[n, k - 1], {"by": (by + k) % nby}) for k in range(1, nby)]
        total = product(halves(src[...].reshape(L * R, C)), (hy[0, by], hy[1, by]))
        for k in range(1, nby):
            copies[k - 1].wait_recv()
            origin = (by + nby - k) % nby
            total += product(halves(ybuf[n, k - 1].reshape(L * R, C)), (hy[0, origin], hy[1, origin]))
        return total

    def flank_start(rows_too, step, src):
        copies = []
        if rows_too:
            for c in range(3):
                for l in range(L):
                    at = c * L + l
                    row_s[step, 0, at:at + 1] = src[c, l, 0:1]
                    row_s[step, 1, at:at + 1] = src[c, l, R - 1:R]
            col_s[step] = column_tile([src[c, l] for c in range(3) for l in range(L)])
            if step == 0:
                pl.semaphore_wait(barrier, len(greeted))
            copies.append(push(row_s.at[step, 1], row_r.at[step, 0], {"bx": (bx + 1) % nbx}))
            copies.append(push(row_s.at[step, 0], row_r.at[step, 1], {"bx": (bx + nbx - 1) % nbx}))
            tile, land = col_s.at[step], col_r
        else:
            for l in range(L):
                pr_s[step, 0, l:l + 1] = src[l, 0:1]
                pr_s[step, 1, l:l + 1] = src[l, R - 1:R]
            copies.append(push(pr_s.at[step, 1], pr_r.at[step, 0], {"bx": (bx + 1) % nbx}))
            copies.append(push(pr_s.at[step, 0], pr_r.at[step, 1], {"bx": (bx + nbx - 1) % nbx}))
            pc_s[step] = column_tile([src[l] for l in range(L)])
            tile, land = pc_s.at[step], pc_r
        copies.append(push(tile, land.at[step, 0], {"by": (by + 1) % nby}))
        copies.append(push(tile, land.at[step, 1], {"by": (by + nby - 1) % nby}))
        return copies

    for step in range(STEPS):
        src = p_in if step == 0 else p_mid
        flanks = flank_start(True, step, src)
        if step == 0:
            lateral = lam[...]
            previous = None
            for l in range(L):
                pivot = perm[l] * lateral + inter[l] + inter[l + 1]
                if l:
                    pivot = pivot - inter[l] * previous
                inverse = 1.0 / pivot
                coef[l] = inverse
                previous = inter[l + 1] * inverse
                ratio[l] = previous
        for copy in flanks:
            copy.wait_recv()
        low_col = col_r[step, 0]
        high_col = col_r[step, 1]

        def edges(c, l):
            at = c * L + l
            return (row_r[step, 0, at:at + 1], row_r[step, 1, at:at + 1],
                    low_col[:, C // 2 + at:C // 2 + at + 1], high_col[:, at:at + 1])

        zero = jnp.zeros((R, C), jnp.float32)
        for l in range(L):
            low, high, _, _ = edges(0, l)
            _, _, left, right = edges(1, l)
            along_x, along_y = src[0, l], src[1, l]
            above = src[2, l + 1] if l + 1 < L else zero
            below = src[2, l - 1] if l else zero
            q[step, l] = -0.5 * (
                (x_next(along_x, high) - x_prev(along_x, low))
                + (y_next(along_y, right) - y_prev(along_y, left)) + (above - below))
        copies = x_start(q.at[step], 2 * step)
        if step == 0:
            for load in loads:
                load.wait()
        for l in range(L):
            cells = [src[c, l] for c in range(3)]
            squares = [cell * cell for cell in cells]
            whole = squares[0] + squares[1] + squares[2]
            for c in range(3):
                cell, square = cells[c], squares[c]
                low, high, left, right = edges(c, l)
                above = src[c, l + 1] if l + 1 < L else zero
                below = src[c, l - 1] if l else zero
                smooth = stiff[l] * (
                    (x_next(cell, high) + x_prev(cell, low) + y_next(cell, right)
                     + y_prev(cell, left) - 4.0 * cell) + (above + below - 2.0 * cell))
                drive = cell * (
                    2.0 * alpha[l] + 4.0 * landau[0, l] * square
                    + 2.0 * landau[1, l] * (whole - square)
                    + 6.0 * landau[2, l] * (square * square))
                base[c, l] = cell - step_size * (drive - smooth)
        n = 2 * step
        x_mix(copies, n)
        if wide:
            spread(n, step)
            table = (hy[0], hy[1])
            full = jnp.concatenate(
                [z_in[step, j].reshape(L * thin, C) for j in range(nby)], axis=1)
            values = solve(product(halves(full), table), thin)
            full = product(halves(jnp.concatenate(values, axis=0)), table)
            for j in range(nby):
                w_out[step, j] = full[:, j * C:(j + 1) * C].reshape(L, thin, C)
            copies = collect(n + 1, step)
        else:
            x_finish(n, rec_f.at[step])
            for l, value in enumerate(solve(y_pass(rec_f.at[step], n), R)):
                phat[step, l] = value
            u[step] = y_pass(phat.at[step], n + 1).reshape(L, R, C)
            copies = x_start(u.at[step], n + 1)
        x_mix(copies, n + 1)
        x_finish(n + 1, rec_i.at[step])
        flanks = flank_start(False, step, rec_i.at[step])
        last = step == STEPS - 1
        target = p_out if last else p_mid
        for l in range(L):
            above = rec_i[step, l + 1] if l + 1 < L else zero
            below = rec_i[step, l - 1] if l else zero
            along_z = -0.5 * (above - below)
            target[2, l] = base[2, l] + step_size * along_z
            if last:
                f_out[2, l] = along_z
        for copy in flanks:
            copy.wait_recv()
        low_phi = pc_r[step, 0]
        high_phi = pc_r[step, 1]
        for l in range(L):
            phi = rec_i[step, l]
            along_x = -0.5 * (x_next(phi, pr_r[step, 1, l:l + 1])
                              - x_prev(phi, pr_r[step, 0, l:l + 1]))
            along_y = -0.5 * (y_next(phi, high_phi[:, l:l + 1])
                              - y_prev(phi, low_phi[:, C // 2 + l:C // 2 + l + 1]))
            target[0, l] = base[0, l] + step_size * along_x
            target[1, l] = base[1, l] + step_size * along_y
            if last:
                f_out[0, l] = along_x
                f_out[1, l] = along_y
    for wait in sends:
        wait()


def shards(polarization, alpha_field, landau, stiffness, permittivity, interfaces):
    _, L, R, C = polarization.shape
    nbx = lax.axis_size("bx")
    nby = lax.axis_size("by")
    bx = lax.axis_index("bx")
    by = lax.axis_index("by")
    rep = max(1, nbx // L)
    lp = max(1, L // nbx)
    own = nbx // rep
    grid_x, grid_y = nbx * R, nby * C
    wide = is_wide(R, nbx, nby, L)
    pool = np if wide else jnp
    make = fixed_table if wide else cas_table
    line = pool.arange(R, dtype=jnp.int32)
    owners = pool.arange(own, dtype=jnp.int32)
    if not wide:
        owners = owners + bx % rep * own
    wanted = (owners[:, None] * R + line[None, :]).reshape(own * R, 1)
    hx = make(wanted, pool.arange(grid_x, dtype=jnp.int32)[None, :], grid_x)
    every_col = pool.arange(grid_y, dtype=jnp.int32)
    my_rows = bx * R + jnp.arange(R, dtype=jnp.int32)
    my_cols = by * C + jnp.arange(C, dtype=jnp.int32)
    if wide:
        hy = make(every_col[:, None], every_col[None, :], grid_y)
        my_rows = bx * R + by * (R // nby) + jnp.arange(R // nby, dtype=jnp.int32)
        my_cols = jnp.arange(grid_y, dtype=jnp.int32)
    else:
        hy = make(every_col[:, None], my_cols[None, :], grid_y).reshape(2, nby, C, C)
    wave_x = jnp.sin(jnp.pi * my_rows.astype(jnp.float32) / grid_x)
    wave_y = jnp.sin(jnp.pi * my_cols.astype(jnp.float32) / grid_y)
    lam = 4.0 * wave_x[:, None] ** 2 + 4.0 * wave_y[None, :] ** 2
    sizes = (L, R, C, nbx, nby, rep, lp, own)
    n_copies = STEPS * (8 + 2 * (nbx * nby + own if wide else nbx + own + nby))
    f32 = jnp.float32
    vmem = pl.BlockSpec(memory_space=pltpu.VMEM)
    hbm = pl.BlockSpec(memory_space=pltpu.HBM)
    smem = pl.BlockSpec(memory_space=pltpu.SMEM)
    S = STEPS
    scratch = [
        pltpu.VMEM((3, L, R, C), f32), pltpu.VMEM((3, L, R, C), f32),
        pltpu.VMEM((L,) + lam.shape, f32), pltpu.VMEM((L,) + lam.shape, f32),
        pltpu.VMEM((S, L, R, C), f32), pltpu.VMEM((2 * S, lp, grid_x, C), f32),
        pltpu.VMEM((2 * S, own, lp, R, C), f32), pltpu.VMEM((S, L, R, C), f32),
        pltpu.VMEM((S, 2, 3 * L, C), f32), pltpu.VMEM((S, 2, 3 * L, C), f32),
        pltpu.VMEM((S, R, C), f32), pltpu.VMEM((S, 2, R, C), f32),
        pltpu.VMEM((S, 2, L, C), f32), pltpu.VMEM((S, 2, L, C), f32),
        pltpu.VMEM((S, R, C), f32), pltpu.VMEM((S, 2, R, C), f32),
        pltpu.SemaphoreType.DMA((n_copies,)), pltpu.SemaphoreType.DMA((n_copies,)),
        pltpu.VMEM((L, R, C), f32), pltpu.VMEM(hx.shape, hx.dtype),
        pltpu.VMEM(hy.shape, hy.dtype), pltpu.SemaphoreType.DMA((3,)),
    ]
    if wide:
        thin = (S, nby, L, R // nby, C)
        scratch += [pltpu.VMEM(thin, f32), pltpu.VMEM(thin, f32)]
    else:
        scratch += [
            pltpu.VMEM((S, L, R, C), f32), pltpu.VMEM((2 * S, nby - 1, L, R, C), f32),
            pltpu.VMEM((S, L, R, C), f32), pltpu.VMEM((S, L, R, C), f32),
        ]
    out = jax.ShapeDtypeStruct(polarization.shape, f32)
    return pl.pallas_call(
        functools.partial(kernel, sizes),
        out_shape=(out, out),
        in_specs=[vmem, hbm, smem, smem, smem, smem, vmem, hbm, hbm],
        out_specs=(vmem, vmem),
        scratch_shapes=scratch,
        compiler_params=pltpu.CompilerParams(
            collective_id=0, has_side_effects=True, vmem_limit_bytes=48 * 1024 * 1024),
    )(polarization, alpha_field, landau, stiffness, permittivity, interfaces, lam, hx, hy)


def solution(mesh):
    return jax.shard_map(
        shards,
        mesh=mesh,
        in_specs=(P(None, None, "bx", "by"), P(None, "bx", "by"), P(), P(), P(), P()),
        out_specs=(P(None, None, "bx", "by"), P(None, None, "bx", "by")),
        check_vma=False,
    )
```

```python
import functools

import jax
import jax.numpy as jnp
import numpy as np
from jax import lax
from jax.experimental import pallas as pl
from jax.experimental.pallas import tpu as pltpu
from jax.sharding import PartitionSpec as P

STEPS = 2
step_size = 0.05
MESH = pl.DeviceIdType.MESH
PAD = 8


def cas_table(left, right, length):
    turns = left * right % length
    angle = 2.0 * jnp.pi / length * turns.astype(jnp.float32)
    table = jnp.cos(angle) + jnp.sin(angle)
    high = lax.reduce_precision(table, 8, 7)
    return jnp.stack([high.astype(jnp.bfloat16), (table - high).astype(jnp.bfloat16)])


def fixed_table(left, right, length):
    angle = 2.0 * np.pi / length * (left * right % length)
    table = (np.cos(angle) + np.sin(angle)).astype(np.float32)
    high = table.astype(jnp.bfloat16)
    low = (table - high.astype(np.float32)).astype(jnp.bfloat16)
    return jnp.asarray(np.stack([high, low]))


def is_wide(rows, nbx, nby, layers):
    return layers % nbx == 0 and rows % (8 * nby) == 0


def halves(value):
    high = value.astype(jnp.bfloat16)
    low = (value - high.astype(jnp.float32)).astype(jnp.bfloat16)
    return high, low


def product(left, right):
    dot = functools.partial(jnp.dot, preferred_element_type=jnp.float32)
    return dot(left[0], right[0]) + (dot(left[0], right[1]) + dot(left[1], right[0]))


def kernel(sizes, p_in, alpha_h, landau, stiff, perm, inter, lam, hx_h, hy_h, p_out, f_out, *scratch):
    L, R, C, nbx, nby, rep, lp, own = sizes
    (p_mid, base, coef, ratio, q, inb, outs, rec_i,
     row_s, row_r, col_s, col_r, pc_s, pc_r, ssem, rsem,
     alpha, hx, hy, local_sem) = scratch[:20]
    wide = is_wide(R, nbx, nby, L)
    if wide:
        z_in, w_out = scratch[20:]
    else:
        rec_f, ybuf, phat, u = scratch[20:]
    thin = R // nby
    R2 = R + PAD
    bx = lax.axis_index("bx")
    by = lax.axis_index("by")
    group = bx // rep
    part = bx % rep
    scale = 1.0 / (R * nbx * C * nby)
    loads = [pltpu.make_async_copy(src, dst, local_sem.at[at]) for at, (src, dst) in
             enumerate(((alpha_h, alpha), (hx_h, hx), (hy_h, hy)))]
    for load in loads:
        load.start()
    slots = [0]
    sends = []

    barrier = pltpu.get_barrier_semaphore()
    others = [(a, b) for b in range(nby) for a in range(nbx) if a or b]
    greeted = [(a, b) for a, b in others if wide or not a or not b]
    for a, b in greeted:
        pl.semaphore_signal(
            barrier, inc=1, device_id={"bx": (bx + a) % nbx, "by": (by + b) % nby},
            device_id_type=MESH)

    def remote(src, dst, device, slot):
        return pltpu.make_async_remote_copy(
            src_ref=src, dst_ref=dst, send_sem=ssem.at[slot], recv_sem=rsem.at[slot],
            device_id=device, device_id_type=MESH)

    def fresh():
        slots[0] += 1
        return slots[0] - 1

    def push(src, dst, device):
        copy = remote(src, dst, device, fresh())
        copy.start()
        sends.append(copy.wait_send)
        return copy

    rows = lax.broadcasted_iota(jnp.int32, (R, C), 0)
    lanes = lax.broadcasted_iota(jnp.int32, (R, C), 1)

    def x_next(f, high):
        return jnp.where(rows == R - 1, high, pltpu.roll(f, R - 1, 0))

    def x_prev(f, low):
        return jnp.where(rows == 0, low, pltpu.roll(f, 1, 0))

    def y_next(f, high):
        return jnp.where(lanes == C - 1, high, pltpu.roll(f, C - 1, 1))

    def y_prev(f, low):
        return jnp.where(lanes == 0, low, pltpu.roll(f, 1, 1))

    def column_tile(blocks):
        tile = jnp.zeros((R, C), jnp.float32)
        for at, block in enumerate(blocks):
            tile = jnp.where(lanes == at, block[:, 0:1], tile)
            tile = jnp.where(lanes == C // 2 + at, block[:, C - 1:C], tile)
        return tile

    def x_start(src, n):
        mine = inb.at[n, :, pl.ds(pl.multiple_of(bx * R, R), R)]
        copies = []
        for k in range(1, nbx):
            to = (bx + k) % nbx
            copies.append(push(src.at[pl.ds(to // rep * lp, lp)], mine, {"bx": to}))
        for layer in range(lp):
            inb[n, layer, pl.ds(pl.multiple_of(bx * R, R), R)] = src[group * lp + layer]
        return copies

    def x_mix(copies, n):
        for copy in copies:
            copy.wait_recv()
        table = (hx[0], hx[1])
        for layer in range(lp):
            outs[n, :, layer] = product(table, halves(inb[n, layer])).reshape(own, R2, C)

    def spread(n, step):
        copies = []
        for a, b in others:
            to_x, to_y = (bx + a) % nbx, (by + b) % nby
            copies.append(push(
                outs.at[n, to_x, :, pl.ds(pl.multiple_of(to_y * thin, thin), thin)],
                z_in.at[step, by, pl.ds(bx * lp, lp)], {"bx": to_x, "by": to_y}))
        for layer in range(lp):
            z_in[step, by, bx * lp + layer] = outs[
                n, bx, layer, pl.ds(pl.multiple_of(by * thin, thin), thin)]
        for copy in copies:
            copy.wait_recv()

    def collect(n, step):
        at = pl.ds(pl.multiple_of(bx * R + by * thin, thin), thin)
        copies = []
        for a, b in others:
            to_x, to_y = (bx + a) % nbx, (by + b) % nby
            copies.append(push(
                w_out.at[step, to_y, pl.ds(to_x * lp, lp)], inb.at[n, :, at],
                {"bx": to_x, "by": to_y}))
        for layer in range(lp):
            inb[n, layer, at] = w_out[step, by, bx * lp + layer]
        return copies

    def solve(spectrum, height):
        primes = []
        for l in range(L):
            source = spectrum[l * height:(l + 1) * height] * scale
            if l:
                source = source + inter[l] * primes[-1]
            primes.append(source * coef[l])
        values = [primes[-1]]
        for l in range(L - 2, -1, -1):
            values.insert(0, primes[l] + ratio[l] * values[0])
        return values

    def x_finish(n, dst, height):
        waits = []
        landing = dst.at[pl.ds(group * lp, lp)]
        for t in range(own):
            local = (group + t) % own
            to = part * own + local
            src = outs.at[n, local, :, pl.ds(0, height)]
            if rep == 1:
                if t == 0:
                    continue
                waits.append(push(src, landing, {"bx": to}).wait_recv)
                continue
            slot = fresh()

            def go(src=src, to=to, slot=slot):
                remote(src, landing, {"bx": to}, slot).start()

            def gone(src=src, to=to, slot=slot):
                @pl.when(to != bx)
                def _():
                    remote(src, landing, {"bx": to}, slot).wait_send()

            def came(src=src, to=to, slot=slot, t=t):
                origin = (bx % own + own - t) % own * rep + bx // own

                @pl.when(origin != bx)
                def _():
                    remote(src, landing, {"bx": to}, slot).wait_recv()

            pl.when(to != bx)(go)
            sends.append(gone)
            waits.append(came)

        def keep():
            for layer in range(lp):
                dst[group * lp + layer] = outs[n, bx % own, layer, 0:height]

        if rep == 1:
            keep()
        else:
            pl.when(bx // own == part)(keep)
        for wait in waits:
            wait()

    def y_pass(src, n):
        copies = [push(src, ybuf.at[n, k - 1], {"by": (by + k) % nby}) for k in range(1, nby)]
        total = product(halves(src[...].reshape(L * R, C)), (hy[0, by], hy[1, by]))
        for k in range(1, nby):
            copies[k - 1].wait_recv()
            origin = (by + nby - k) % nby
            total += product(halves(ybuf[n, k - 1].reshape(L * R, C)), (hy[0, origin], hy[1, origin]))
        return total

    def flank_start(rows_too, step, src):
        copies = []
        if rows_too:
            for c in range(3):
                for l in range(L):
                    at = c * L + l
                    row_s[step, 0, at:at + 1] = src[c, l, 0:1]
                    row_s[step, 1, at:at + 1] = src[c, l, R - 1:R]
            col_s[step] = column_tile([src[c, l] for c in range(3) for l in range(L)])
            if step == 0:
                pl.semaphore_wait(barrier, len(greeted))
            copies.append(push(row_s.at[step, 1], row_r.at[step, 0], {"bx": (bx + 1) % nbx}))
            copies.append(push(row_s.at[step, 0], row_r.at[step, 1], {"bx": (bx + nbx - 1) % nbx}))
            tile, land = col_s.at[step], col_r
        else:
            pc_s[step] = column_tile([src[l, 0:R] for l in range(L)])
            tile, land = pc_s.at[step], pc_r
        copies.append(push(tile, land.at[step, 0], {"by": (by + 1) % nby}))
        copies.append(push(tile, land.at[step, 1], {"by": (by + nby - 1) % nby}))
        return copies

    for step in range(STEPS):
        src = p_in if step == 0 else p_mid
        flanks = flank_start(True, step, src)
        if step == 0:
            lateral = lam[...]
            previous = None
            for l in range(L):
                pivot = perm[l] * lateral + inter[l] + inter[l + 1]
                if l:
                    pivot = pivot - inter[l] * previous
                inverse = 1.0 / pivot
                coef[l] = inverse
                previous = inter[l + 1] * inverse
                ratio[l] = previous
        for copy in flanks:
            copy.wait_recv()
        low_col = col_r[step, 0]
        high_col = col_r[step, 1]

        def edges(c, l):
            at = c * L + l
            return (row_r[step, 0, at:at + 1], row_r[step, 1, at:at + 1],
                    low_col[:, C // 2 + at:C // 2 + at + 1], high_col[:, at:at + 1])

        zero = jnp.zeros((R, C), jnp.float32)
        for l in range(L):
            low, high, _, _ = edges(0, l)
            _, _, left, right = edges(1, l)
            along_x, along_y = src[0, l], src[1, l]
            above = src[2, l + 1] if l + 1 < L else zero
            below = src[2, l - 1] if l else zero
            q[step, l] = -0.5 * (
                (x_next(along_x, high) - x_prev(along_x, low))
                + (y_next(along_y, right) - y_prev(along_y, left)) + (above - below))
        copies = x_start(q.at[step], 2 * step)
        if step == 0:
            for load in loads:
                load.wait()
        for l in range(L):
            cells = [src[c, l] for c in range(3)]
            squares = [cell * cell for cell in cells]
            whole = squares[0] + squares[1] + squares[2]
            for c in range(3):
                cell, square = cells[c], squares[c]
                low, high, left, right = edges(c, l)
                above = src[c, l + 1] if l + 1 < L else zero
                below = src[c, l - 1] if l else zero
                smooth = stiff[l] * (
                    (x_next(cell, high) + x_prev(cell, low) + y_next(cell, right)
                     + y_prev(cell, left) - 4.0 * cell) + (above + below - 2.0 * cell))
                drive = cell * (
                    2.0 * alpha[l] + 4.0 * landau[0, l] * square
                    + 2.0 * landau[1, l] * (whole - square)
                    + 6.0 * landau[2, l] * (square * square))
                base[c, l] = cell - step_size * (drive - smooth)
        n = 2 * step
        x_mix(copies, n)
        if wide:
            spread(n, step)
            table = (hy[0], hy[1])
            full = jnp.concatenate(
                [z_in[step, j].reshape(L * thin, C) for j in range(nby)], axis=1)
            values = solve(product(halves(full), table), thin)
            full = product(halves(jnp.concatenate(values, axis=0)), table)
            for j in range(nby):
                w_out[step, j] = full[:, j * C:(j + 1) * C].reshape(L, thin, C)
            copies = collect(n + 1, step)
        else:
            x_finish(n, rec_f.at[step], R)
            for l, value in enumerate(solve(y_pass(rec_f.at[step], n), R)):
                phat[step, l] = value
            u[step] = y_pass(phat.at[step], n + 1).reshape(L, R, C)
            copies = x_start(u.at[step], n + 1)
        x_mix(copies, n + 1)
        x_finish(n + 1, rec_i.at[step], R2)
        flanks = flank_start(False, step, rec_i.at[step])
        last = step == STEPS - 1
        target = p_out if last else p_mid
        for l in range(L):
            phi = rec_i[step, l, 0:R]
            low = rec_i[step, l, R:R + 1]
            high = rec_i[step, l, R + 1:R + 2]
            along_x = -0.5 * (x_next(phi, high) - x_prev(phi, low))
            above = rec_i[step, l + 1, 0:R] if l + 1 < L else zero
            below = rec_i[step, l - 1, 0:R] if l else zero
            along_z = -0.5 * (above - below)
            target[0, l] = base[0, l] + step_size * along_x
            target[2, l] = base[2, l] + step_size * along_z
            if last:
                f_out[0, l] = along_x
                f_out[2, l] = along_z
        for copy in flanks:
            copy.wait_recv()
        low_phi = pc_r[step, 0]
        high_phi = pc_r[step, 1]
        for l in range(L):
            phi = rec_i[step, l, 0:R]
            along_y = -0.5 * (y_next(phi, high_phi[:, l:l + 1])
                              - y_prev(phi, low_phi[:, C // 2 + l:C // 2 + l + 1]))
            target[1, l] = base[1, l] + step_size * along_y
            if last:
                f_out[1, l] = along_y
    for wait in sends:
        wait()


def shards(polarization, alpha_field, landau, stiffness, permittivity, interfaces):
    _, L, R, C = polarization.shape
    nbx = lax.axis_size("bx")
    nby = lax.axis_size("by")
    bx = lax.axis_index("bx")
    by = lax.axis_index("by")
    rep = max(1, nbx // L)
    lp = max(1, L // nbx)
    own = nbx // rep
    grid_x, grid_y = nbx * R, nby * C
    R2 = R + PAD
    wide = is_wide(R, nbx, nby, L)
    pool = np if wide else jnp
    make = fixed_table if wide else cas_table
    line = pool.arange(R2, dtype=jnp.int32)
    line = pool.where(line < R, line, pool.where(line == R, -1, R))
    owners = pool.arange(own, dtype=jnp.int32)
    if not wide:
        owners = owners + bx % rep * own
    wanted = ((owners[:, None] * R + line[None, :] + grid_x) % grid_x).reshape(own * R2, 1)
    hx = make(wanted, pool.arange(grid_x, dtype=jnp.int32)[None, :], grid_x)
    every_col = pool.arange(grid_y, dtype=jnp.int32)
    my_rows = bx * R + jnp.arange(R, dtype=jnp.int32)
    my_cols = by * C + jnp.arange(C, dtype=jnp.int32)
    if wide:
        hy = make(every_col[:, None], every_col[None, :], grid_y)
        my_rows = bx * R + by * (R // nby) + jnp.arange(R // nby, dtype=jnp.int32)
        my_cols = jnp.arange(grid_y, dtype=jnp.int32)
    else:
        hy = make(every_col[:, None], my_cols[None, :], grid_y).reshape(2, nby, C, C)
    wave_x = jnp.sin(jnp.pi * my_rows.astype(jnp.float32) / grid_x)
    wave_y = jnp.sin(jnp.pi * my_cols.astype(jnp.float32) / grid_y)
    lam = 4.0 * wave_x[:, None] ** 2 + 4.0 * wave_y[None, :] ** 2
    sizes = (L, R, C, nbx, nby, rep, lp, own)
    n_copies = STEPS * (6 + 2 * (nbx * nby + own if wide else nbx + own + nby))
    f32 = jnp.float32
    vmem = pl.BlockSpec(memory_space=pltpu.VMEM)
    hbm = pl.BlockSpec(memory_space=pltpu.HBM)
    smem = pl.BlockSpec(memory_space=pltpu.SMEM)
    S = STEPS
    scratch = [
        pltpu.VMEM((3, L, R, C), f32), pltpu.VMEM((3, L, R, C), f32),
        pltpu.VMEM((L,) + lam.shape, f32), pltpu.VMEM((L,) + lam.shape, f32),
        pltpu.VMEM((S, L, R, C), f32), pltpu.VMEM((2 * S, lp, grid_x, C), f32),
        pltpu.VMEM((2 * S, own, lp, R2, C), f32), pltpu.VMEM((S, L, R2, C), f32),
        pltpu.VMEM((S, 2, 3 * L, C), f32), pltpu.VMEM((S, 2, 3 * L, C), f32),
        pltpu.VMEM((S, R, C), f32), pltpu.VMEM((S, 2, R, C), f32),
        pltpu.VMEM((S, R, C), f32), pltpu.VMEM((S, 2, R, C), f32),
        pltpu.SemaphoreType.DMA((n_copies,)), pltpu.SemaphoreType.DMA((n_copies,)),
        pltpu.VMEM((L, R, C), f32), pltpu.VMEM(hx.shape, hx.dtype),
        pltpu.VMEM(hy.shape, hy.dtype), pltpu.SemaphoreType.DMA((3,)),
    ]
    if wide:
        thin = (S, nby, L, R // nby, C)
        scratch += [pltpu.VMEM(thin, f32), pltpu.VMEM(thin, f32)]
    else:
        scratch += [
            pltpu.VMEM((S, L, R, C), f32), pltpu.VMEM((2 * S, nby - 1, L, R, C), f32),
            pltpu.VMEM((S, L, R, C), f32), pltpu.VMEM((S, L, R, C), f32),
        ]
    out = jax.ShapeDtypeStruct(polarization.shape, f32)
    return pl.pallas_call(
        functools.partial(kernel, sizes),
        out_shape=(out, out),
        in_specs=[vmem, hbm, smem, smem, smem, smem, vmem, hbm, hbm],
        out_specs=(vmem, vmem),
        scratch_shapes=scratch,
        compiler_params=pltpu.CompilerParams(
            collective_id=0, has_side_effects=True, vmem_limit_bytes=65 * 1000 * 1000),
    )(polarization, alpha_field, landau, stiffness, permittivity, interfaces, lam, hx, hy)


def solution(mesh):
    return jax.shard_map(
        shards,
        mesh=mesh,
        in_specs=(P(None, None, "bx", "by"), P(None, "bx", "by"), P(), P(), P(), P()),
        out_specs=(P(None, None, "bx", "by"), P(None, None, "bx", "by")),
        check_vma=False,
    )
```
